32 devices in a mesh: groups: 2 (over y), cubes: 16 (over z, x, core).
Axes of the slice: x: 2, y: 2, z: 4, core: 2. Of those that a mesh axis runs over, the one named last changes fastest.
Arguments:
- query_rows: bfloat16 [4096, 2560], P(('groups', 'cubes')), parts along dimension 0, may hold values from -8 to 8
- key_rows: bfloat16 [4096, 2560], P(('groups', 'cubes')), parts along dimension 0, may hold values from -9 to 9
- value_rows: bfloat16 [4096, 2560], P(('groups', 'cubes')), parts along dimension 0, may hold values from -6 to 6
- gate_logits: bfloat16 [4096, 40], P(('groups', 'cubes')), parts along dimension 0, may hold values from -6 to 6
- selection: int32 [64, 20, 8], P('groups'), parts along dimension 0, may hold values from 0 to 31, all different within a row; in each aligned block of 40 rows (0 to 39, 40 to 79, ..., all dimensions but the last counted through in order) at most 11 rows name the same one
- cube_ids: int32 [64], P('groups'), parts along dimension 0, may hold values from 0 to 31, each once
Outputs:
- mixed: bfloat16 [4096, 2560], P(('groups', 'cubes')), parts along dimension 0
The draws below stay inside these ranges and needn't reach their ends.
There are 2 independent parts, one for each index of `groups`. The reference program is written for one: setup_inputs(seed, part) draws one part's arguments, and reference() takes and returns one part's arrays. A program takes and returns all parts, laid end to end along the dimension named above; each array names one. Nothing has to cross between parts.
Inputs may be any that keep to these rules, and one draw needn't show every extreme that they name: `selection`: each row of 8 names different cubes. Among the rows of one device (its 2 stored blocks with all 20 heads) no cube is named more than 11 times, a bound that some block reaches. `cube_ids`: each cube number appears once.
All inputs are finite; a program needn't handle non-finite values.
Results may differ from the reference program's by a relative error of at most 0.0047.
Values may be sent and summed in bfloat16 or wider, within the bound.
No kernel may reach another device: no remote copies, remote signals or barrier semaphores. Data moves between devices by JAX's collectives and lax.ppermute only.
A program may use at most 128 MiB of HBM per device.

```python
import math
import jax
import jax.numpy as jnp
import numpy as np
from jax import lax

HEADS = 20
HDIM = 128
CUBE = 64
TOPK = 8
CUBE_DEV = 2
NC = 32
TOKENS = 2048
MOST = 11


def shared_part(key, salt):
    cube_key, token_key = jax.random.split(jax.random.fold_in(key, salt))
    shared = jnp.clip(jax.random.normal(cube_key, (NC, 1, HEADS * HDIM), jnp.float32), -4.0, 4.0) * 0.8
    return (shared, token_key)


def cube_rows(key, salt):
    shared, token_key = shared_part(key, salt)
    single = jnp.clip(jax.random.normal(token_key, (NC, CUBE, HEADS * HDIM), jnp.float32), -4.0, 4.0) * 0.6
    return shared + single


def draw_key_rows(key, part):
    values = cube_rows(key, 11)
    return values.reshape(TOKENS, HEADS * HDIM).astype(jnp.bfloat16)


def draw_value_rows(key, part):
    values = cube_rows(key, 17)
    return values.reshape(TOKENS, HEADS * HDIM).astype(jnp.bfloat16)


def draw_query_rows(key, part):
    normal_key = jax.random.fold_in(jax.random.fold_in(key, 13), 0)
    noise = jnp.clip(jax.random.normal(normal_key, (NC, CUBE, HEADS * HDIM), jnp.float32), -4.0, 4.0) * 0.7
    key_shared, unused = shared_part(key, 11)
    earlier = jnp.roll(key_shared, CUBE_DEV, axis=0)
    values = (noise + 1.5 * earlier).reshape(TOKENS, HEADS * HDIM)
    return values.astype(jnp.bfloat16)


def block_levels(key, dims, pieces, low, high):
    def one(dim, blocks):
        heights = jax.random.uniform(jax.random.fold_in(jax.random.fold_in(key, 6), dim), (blocks,), jnp.float32, low / len(pieces), high / len(pieces))
        return jnp.repeat(jnp.exp(heights), dims[dim] // blocks).reshape((-1,) + (1,) * (len(dims) - dim - 1))

    level = one(*pieces[0])
    for cut in pieces[1:]:
        level = level * one(*cut)
    return level


def deal_out(stream_key, own, number, rows, amount, top, most, slope):
    order = jax.random.permutation(stream_key, amount)
    crowded, common = load_shares(amount, rows * top, most, slope, True), load_shares(amount, rows * top, most, slope, False)
    places = jnp.arange(amount)

    def named(lengths, turn):
        used = int((lengths > 0).sum())
        fixed = max(1, used // 4)
        shifted = fixed + (places - fixed + turn * (used - fixed)) % max(1, amount - fixed)
        return jnp.zeros((amount,), jnp.int32).at[order[jnp.where(places < fixed, places, shifted)]].set(jnp.asarray(lengths, jnp.int32))

    lengths = jnp.where(number % 4 == 0, named(crowded, number // 4), named(common, number - number // 4 - 1))
    mixed = jax.random.permutation(jax.random.fold_in(own, 3), amount)
    source_of, sink = mixed[0:amount // 2 * 2:2], mixed[1:amount // 2 * 2:2]
    slack = jnp.minimum(lengths[source_of] - 1, most - lengths[sink]) // 2
    slack = jnp.where((source_of == order[0]) | (sink == order[0]) | (lengths[sink] == 0), 0, jnp.maximum(slack, 0))
    shifted = jax.random.randint(jax.random.fold_in(own, 4), (amount // 2,), 0, 1 << 20) % (slack + 1)
    lengths = lengths.at[source_of].add(-shifted).at[sink].add(shifted)
    items = jnp.searchsorted(jnp.cumsum(lengths), jnp.arange(rows * top), side="right").astype(jnp.int32)
    table = items.reshape(top, rows).T
    table = table[jax.random.permutation(jax.random.fold_in(own, 1), rows)]
    turn = jax.random.randint(jax.random.fold_in(own, 2), (rows, 1), 0, top)
    return jnp.take_along_axis(table, (jnp.arange(top)[None, :] + turn) % top, axis=1)


def load_shares(amount, total, reach, skew, full):
    loads = [(1 << 20) // math.isqrt(rank ** skew) + 1 for rank in range(1, amount + 1)]
    largest = reach if full else min(reach, max(-(-total // amount), total * loads[0] // sum(loads)))
    least = 1 if total - largest >= amount - 1 else 0
    holding, rest = [largest] + [least] * (amount - 1), total - largest - least * (amount - 1)
    while rest > 0:
        free = [i for i in range(1, amount) if holding[i] < largest] or [i for i in range(1, amount) if holding[i] < reach]
        whole, budget = sum([loads[i] for i in free]), rest
        for i in free:
            extra = min(reach - holding[i], max(1, budget * loads[i] // whole), rest)
            holding[i] = holding[i] + extra
            rest = rest - extra
    return np.array(holding)


def gaussian(key, dims, deviation, bound, pieces=(), held_as=jnp.bfloat16):
    entries = deviation * jax.random.normal(key, dims, jnp.float32)
    if pieces:
        entries = entries * block_levels(key, dims, pieces, -0.22, 0.18)
    return jnp.clip(entries, -bound, bound).astype(held_as)


def setup_inputs(seed: int = 0, part: int = 0) -> dict:
    streams_of = jax.random.split(jax.random.key(seed), 7)
    own_keys = jax.random.split(jax.random.fold_in(streams_of[6], part), 7)
    query_rows = draw_query_rows(jax.random.fold_in(jax.random.fold_in(streams_of[6], part), 71), part)
    key_rows = draw_key_rows(jax.random.fold_in(jax.random.fold_in(streams_of[6], part), 71), part)
    value_rows = draw_value_rows(jax.random.fold_in(jax.random.fold_in(streams_of[6], part), 71), part)
    gate_logits = gaussian(own_keys[3], (TOKENS, 2 * HEADS), 1.5, 6.0, ((0, 16),))
    selection_keys = jax.random.split(jax.random.fold_in(own_keys[4], 1), NC * HEADS // (CUBE_DEV * HEADS))
    selection_turns = jax.random.permutation(jax.random.fold_in(own_keys[4], 3), NC * HEADS // (CUBE_DEV * HEADS))
    selection = jax.vmap(lambda own, number: deal_out(jax.random.fold_in(own_keys[4], 2), own, number, CUBE_DEV * HEADS, NC, TOPK, MOST, 2))(selection_keys, selection_turns).reshape((NC, HEADS, TOPK))
    cube_ids = jax.random.permutation(own_keys[5], NC).astype(jnp.int32)
    return {"query_rows": query_rows, "key_rows": key_rows, "value_rows": value_rows, "gate_logits": gate_logits, "selection": selection, "cube_ids": cube_ids}


def reference(query_rows, key_rows, value_rows, gate_logits, selection, cube_ids):
    factor = 1.0 / math.sqrt(HDIM)
    feature_width = HEADS * HDIM
    pooled_key = lax.optimization_barrier(jnp.mean(key_rows.astype(jnp.float32).reshape(NC, CUBE, feature_width), axis=1)).astype(jnp.bfloat16)
    pooled_value = lax.optimization_barrier(jnp.mean(value_rows.astype(jnp.float32).reshape(NC, CUBE, feature_width), axis=1)).astype(jnp.bfloat16)
    pooled_keys = lax.optimization_barrier(pooled_key).astype(jnp.float32).reshape(NC, HEADS, HDIM)
    pooled_values = lax.optimization_barrier(pooled_value).astype(jnp.float32).reshape(NC, HEADS, HDIM)
    query_blocks = query_rows.reshape(NC, CUBE, HEADS, HDIM)
    key_blocks = key_rows.reshape(NC, CUBE, HEADS, HDIM).transpose(0, 2, 1, 3)
    value_blocks = value_rows.reshape(NC, CUBE, HEADS, HDIM).transpose(0, 2, 1, 3)
    cube_range = jnp.arange(NC, dtype=jnp.int32)
    position = lax.optimization_barrier(jnp.sum(jnp.where(cube_ids[None, :] == cube_range[:, None], cube_range[None, :], 0), axis=1)).astype(jnp.int32)
    targets = jnp.take(position, selection.reshape(-1)).reshape(NC, HEADS, TOPK).astype(jnp.int32)
    head_range = jnp.arange(HEADS, dtype=jnp.int32)

    def one_block(inputs):
        queries, chosen = inputs
        query_float = queries.astype(jnp.float32)
        coarse_scores = jnp.einsum('thd,jhd->htj', query_float, pooled_keys) * factor
        coarse_weights = jnp.exp(coarse_scores - lax.optimization_barrier(jnp.max(coarse_scores, axis=2, keepdims=True)))
        coarse_rounded = lax.optimization_barrier(coarse_weights.astype(jnp.bfloat16)).astype(jnp.float32)
        coarse = jnp.einsum('htj,jhd->thd', coarse_rounded, pooled_values)
        coarse = coarse / lax.optimization_barrier(jnp.sum(coarse_weights, axis=2)).T[:, :, None]
        fine_keys = key_blocks[chosen, head_range[:, None]].reshape(HEADS, TOPK * CUBE, HDIM).astype(jnp.float32)
        fine_values = value_blocks[chosen, head_range[:, None]].reshape(HEADS, TOPK * CUBE, HDIM).astype(jnp.float32)
        fine_scores = jnp.einsum('thd,hkd->htk', query_float, fine_keys) * factor
        fine_weights = jnp.exp(fine_scores - lax.optimization_barrier(jnp.max(fine_scores, axis=2, keepdims=True)))
        fine_rounded = lax.optimization_barrier(fine_weights.astype(jnp.bfloat16)).astype(jnp.float32)
        fine = jnp.einsum('htk,hkd->thd', fine_rounded, fine_values)
        fine = fine / lax.optimization_barrier(jnp.sum(fine_weights, axis=2)).T[:, :, None]
        return (coarse, fine)
    coarse, fine = lax.map(one_block, (query_blocks, targets))
    gates = jax.nn.sigmoid(gate_logits.astype(jnp.float32)).reshape(NC, CUBE, 2, HEADS)
    mixed = gates[:, :, 0, :, None] * coarse + gates[:, :, 1, :, None] * fine
    return mixed.reshape(NC * CUBE, feature_width).astype(jnp.bfloat16)
```

```python
import functools
import math

import jax
import jax.numpy as jnp
from jax import lax
from jax.experimental import pallas as pl
from jax.experimental.pallas import tpu as pltpu
from jax.sharding import PartitionSpec as P

CUBE = 64
GATE_ROWS = 8
CHUNKS = (3, 2)
LOG2E = 1.4426950408889634

VMEM = pl.BlockSpec(memory_space=pltpu.VMEM)
SMEM = pl.BlockSpec(memory_space=pltpu.SMEM)
ANY = pl.BlockSpec(memory_space=pl.ANY)


def pack_kernel(spans, width, index_ref, *refs):
    sources = refs[: len(refs) - len(spans)]
    outputs = refs[len(sources) :]
    for (relative, (begin, size)), out in zip(spans, outputs):
        head_group = index_ref[0] ^ relative
        columns = pl.ds(pl.multiple_of(head_group * width + begin, 128), size)
        row = 0
        for source in sources:
            rows = source.shape[0]
            out[row : row + rows, :] = source[:, columns]
            row += rows


def pack(index, sources, spans, width):
    rows = sum(source.shape[0] for source in sources)
    return pl.pallas_call(
        functools.partial(pack_kernel, spans, width),
        out_shape=[jax.ShapeDtypeStruct((rows, size), jnp.bfloat16) for _, (_, size) in spans],
        in_specs=[SMEM] + [VMEM] * len(sources),
        out_specs=[VMEM] * len(spans),
        name="pack",
    )(index, *sources)


def unpack_kernel(spans, width, index_ref, *refs):
    pieces, out = refs[:-1], refs[-1]
    for (relative, (begin, size)), piece in zip(spans, pieces):
        head_group = index_ref[0] ^ relative
        out[:, pl.ds(pl.multiple_of(head_group * width + begin, 128), size)] = piece[...]


def unpack(index, pieces, spans, width, columns):
    return pl.pallas_call(
        functools.partial(unpack_kernel, spans, width),
        out_shape=jax.ShapeDtypeStruct((pieces[0].shape[0], columns), jnp.bfloat16),
        in_specs=[SMEM] + [VMEM] * len(pieces),
        out_specs=VMEM,
        name="unpack",
    )(index, *pieces)


def attend_kernel(shape, tables_ref, *refs):
    groups, local, cubes, heads, first, count, picks, head_size, halves = shape
    queries = refs[:groups]
    stores = refs[groups : groups + halves]
    outs = refs[groups + halves : 2 * groups + halves]
    held, pooled_keys, pooled_values, sems = refs[2 * groups + halves :]
    tokens = local * CUBE
    half_rows = stores[0].shape[0]
    factor = 1.0 / math.sqrt(head_size)

    def copies(head):
        slot = head % 2
        columns = pl.ds(head * head_size, head_size)
        return [
            pltpu.make_async_copy(
                stores[i].at[:, columns],
                held.at[slot, pl.ds(i * half_rows, half_rows), :],
                sems.at[slot, i],
            )
            for i in range(halves)
        ]

    for copy in copies(0):
        copy.start()
    home = tables_ref[cubes + groups * local * heads * picks]
    for head in range(count):
        slot = head % 2
        if head + 1 < count:
            for copy in copies(head + 1):
                copy.start()
        for copy in copies(head):
            copy.wait()
        columns = pl.ds(head * head_size, head_size)

        def pool(piece, carry):
            base = pl.multiple_of(piece * 2 * tokens, 2 * tokens)
            rows = held[slot, pl.ds(base, 2 * tokens), :].astype(jnp.float32)
            means = jnp.sum(rows.reshape(2 * local, CUBE, head_size), axis=1) * (1.0 / CUBE)
            pooled_keys[pl.ds(piece * local, local), :] = means[:local]
            pooled_values[pl.ds(piece * local, local), :] = means[local:]
            return carry

        lax.fori_loop(0, cubes // local, pool, 0)
        coarse_keys = pooled_keys[...].astype(jnp.bfloat16)
        coarse_values = pooled_values[...].astype(jnp.bfloat16)
        for group in range(groups):
            gate_rows = queries[group][tokens : tokens + GATE_ROWS, columns].astype(jnp.float32)
            gates = jnp.transpose(jax.nn.sigmoid(gate_rows))
            for block in range(local):
                rows = slice(block * CUBE, (block + 1) * CUBE)
                query = queries[group][rows, columns]
                base = cubes + (((home ^ group) * local + block) * heads + first + head) * picks
                starts = [
                    pl.multiple_of(tables_ref[tables_ref[base + pick]], CUBE)
                    for pick in range(picks)
                ]
                keys = jnp.concatenate(
                    [held[slot, pl.ds(start, CUBE), :] for start in starts], axis=0
                )
                values = jnp.concatenate(
                    [held[slot, pl.ds(start + tokens, CUBE), :] for start in starts], axis=0
                )

                def part(keys, values):
                    scores = lax.dot_general(
                        query, keys, (((1,), (1,)), ((), ())), preferred_element_type=jnp.float32
                    )
                    top = jnp.max(scores, axis=1, keepdims=True)
                    weights = jnp.exp2((scores - top) * (factor * LOG2E))
                    total = jnp.sum(weights, axis=1, keepdims=True)
                    sums = jnp.dot(
                        weights.astype(jnp.bfloat16), values, preferred_element_type=jnp.float32
                    )
                    return sums, total

                coarse, coarse_total = part(coarse_keys, coarse_values)
                fine, fine_total = part(keys, values)
                mixed = coarse * (gates[rows, 0:1] / coarse_total)
                mixed += fine * (gates[rows, 1:2] / fine_total)
                outs[group][rows, columns] = mixed.astype(jnp.bfloat16)


def attend(tables, queries, stores, local, cubes, heads, first, count, picks, head_size):
    groups, halves = len(queries), len(stores)
    shape = (groups, local, cubes, heads, first, count, picks, head_size, halves)
    tokens = local * CUBE
    out = jax.ShapeDtypeStruct((tokens, count * head_size), jnp.bfloat16)
    units = groups * local * count
    flops = 4 * units * CUBE * CUBE * picks * head_size
    return pl.pallas_call(
        functools.partial(attend_kernel, shape),
        out_shape=[out] * groups,
        in_specs=[SMEM] + [VMEM] * groups + [ANY] * halves,
        out_specs=[VMEM] * groups,
        scratch_shapes=[
            pltpu.VMEM((2, 2 * cubes * CUBE, head_size), jnp.bfloat16),
            pltpu.VMEM((cubes, head_size), jnp.float32),
            pltpu.VMEM((cubes, head_size), jnp.float32),
            pltpu.SemaphoreType.DMA((2, halves)),
        ],
        cost_estimate=pl.CostEstimate(
            flops=flops,
            bytes_accessed=4 * cubes * CUBE * count * head_size,
            transcendentals=units * CUBE * CUBE * picks,
        ),
        name="attend",
    )(tables, *queries, *stores)


def body(query_rows, key_rows, value_rows, gate_logits, selection, cube_ids):
    devices = lax.axis_size("cubes")
    tokens, width = query_rows.shape
    heads_all = gate_logits.shape[1] // 2
    head_size = width // heads_all
    local = tokens // CUBE
    cubes = cube_ids.shape[0]
    picks = selection.shape[2]
    common = math.gcd(heads_all, devices)
    groups = common & -common
    ring = devices // groups
    heads = heads_all // groups
    group_width = heads * head_size
    self_index = lax.axis_index("cubes")
    home = self_index // ring
    place = self_index % ring

    sizes = CHUNKS if sum(CHUNKS) == heads else (heads,)
    firsts = [sum(sizes[:i]) for i in range(len(sizes))]
    spans = [(first * head_size, size * head_size) for first, size in zip(firsts, sizes)]

    def over_groups(value, relative):
        pairs = [(i, i ^ (relative * ring)) for i in range(devices)]
        return lax.ppermute(value, "cubes", pairs)

    def over_ring(value, step):
        return lax.ppermute(value, "cubes", [(i, i ^ step) for i in range(devices)])

    index = home.astype(jnp.int32).reshape(1)
    order = [r for r in range(groups - 1, 1, -1)] + ([1] if groups > 1 else [])
    kv_spans = [(r, span) for span in spans for r in range(groups)]
    kv_sent = pack(index, (key_rows, value_rows), kv_spans, group_width)
    gate_rows = jnp.transpose(gate_logits).reshape(2, heads_all * tokens)
    if tokens != head_size:
        raise ValueError("gate rows")
    gate_rows = jnp.pad(gate_rows, ((0, GATE_ROWS - 2), (0, 0)))
    q_spans = [(r, span) for span in spans for r in range(groups)]
    q_sent = pack(index, (query_rows, gate_rows), q_spans, group_width)

    cube_range = jnp.arange(cubes, dtype=jnp.int32)
    device_of = cube_range // local
    offset = jnp.bitwise_xor(device_of % ring, place)
    steps = [1 << bit for bit in range(ring.bit_length() - 2, -1, -1)]
    slot = jnp.zeros_like(offset)
    for number, step in enumerate(steps):
        slot = slot + jnp.where(jnp.bitwise_and(offset, step) > 0, 1 << number, 0)
    slot = slot * groups + jnp.bitwise_xor(device_of // ring, home)
    start = slot * (2 * tokens) + (cube_range % local) * CUBE
    row_of_cube = jnp.sum(
        jnp.where(cube_ids[None, :] == cube_range[:, None], start[None, :], 0), axis=1
    )
    chosen = selection.reshape(groups, ring, local, heads_all, picks)
    chosen = lax.dynamic_slice(
        chosen, (0, place, 0, home * heads, 0), (groups, 1, local, heads, picks)
    )
    tables = jnp.concatenate((row_of_cube, chosen.reshape(-1), index)).astype(jnp.int32)

    kv_pieces, q_pieces = [], []
    for c in range(len(sizes)):
        kv = list(kv_sent[c * groups : (c + 1) * groups])
        q = list(q_sent[c * groups : (c + 1) * groups])
        for r in order:
            kv[r] = over_groups(kv[r], r)
        for r in order:
            q[r] = over_groups(q[r], r)
        kv_pieces.append(kv)
        q_pieces.append(q)

    out_pieces = []
    for c, (first, size) in enumerate(zip(firsts, sizes)):
        stores = [jnp.concatenate(kv_pieces[c], axis=0)]
        for step in steps:
            gathered = stores[0] if len(stores) == 1 else jnp.concatenate(stores, axis=0)
            stores = [gathered, over_ring(gathered, step)]
        outs = attend(
            tables, q_pieces[c], stores, local, cubes, heads, first, size, picks, head_size
        )
        outs = list(outs)
        for r in order:
            outs[r] = over_groups(outs[r], r)
        out_pieces += outs
    return unpack(index, out_pieces, kv_spans, group_width, width)


def solution(mesh):
    placed = (
        P(("groups", "cubes"), None),
        P(("groups", "cubes"), None),
        P(("groups", "cubes"), None),
        P(("groups", "cubes"), None),
        P("groups", None, None),
        P("groups"),
    )
    return jax.shard_map(
        body, mesh=mesh, in_specs=placed, out_specs=P(("groups", "cubes"), None), check_vma=False
    )
```

```python
import functools
import math

import jax
import jax.numpy as jnp
from jax import lax
from jax.experimental import pallas as pl
from jax.experimental.pallas import tpu as pltpu
from jax.sharding import PartitionSpec as P


CUBE = 64
GATE_ROWS = 8
CHUNKS = (3, 2)
POOL_ROWS = 1024
HELD_BYTES = 8 << 20
LOG2E = 1.4426950408889634

VMEM = pl.BlockSpec(memory_space=pltpu.VMEM)
SMEM = pl.BlockSpec(memory_space=pltpu.SMEM)
ANY = pl.BlockSpec(memory_space=pl.ANY)
TRANSPOSED = (((1,), (1,)), ((), ()))


def pack_kernel(jobs, width, index_ref, *refs):
    sources = refs[: 1 + max(max(rows) for rows, _ in jobs)]
    outputs = iter(refs[len(sources) :])
    for numbers, spans in jobs:
        for relative, begin, size in spans:
            head_group = index_ref[0] ^ relative
            columns = pl.ds(pl.multiple_of(head_group * width + begin, 128), size)
            out, row = next(outputs), 0
            for number in numbers:
                rows = sources[number].shape[0]
                out[row : row + rows, :] = sources[number][:, columns]
                row += rows


def pack(index, jobs, width):
    operands, numbered, shapes = [], [], []
    for sources, spans in jobs:
        numbers = []
        for source in sources:
            known = [i for i, operand in enumerate(operands) if operand is source]
            numbers.append(known[0] if known else len(operands))
            if not known:
                operands.append(source)
        numbered.append((tuple(numbers), tuple(spans)))
        rows = sum(source.shape[0] for source in sources)
        shapes += [jax.ShapeDtypeStruct((rows, size), jnp.bfloat16) for _, _, size in spans]
    return pl.pallas_call(
        functools.partial(pack_kernel, tuple(numbered), width),
        out_shape=shapes,
        in_specs=[SMEM] + [VMEM] * len(operands),
        out_specs=[VMEM] * len(shapes),
        name="pack",
    )(index, *operands)


def unpack_kernel(spans, width, index_ref, *refs):
    pieces, out = refs[:-1], refs[-1]
    for (relative, begin, size), piece in zip(spans, pieces):
        head_group = index_ref[0] ^ relative
        out[:, pl.ds(pl.multiple_of(head_group * width + begin, 128), size)] = piece[...]


def unpack(index, pieces, spans, width, columns):
    return pl.pallas_call(
        functools.partial(unpack_kernel, spans, width),
        out_shape=jax.ShapeDtypeStruct((pieces[0].shape[0], columns), jnp.bfloat16),
        in_specs=[SMEM] + [VMEM] * len(pieces),
        out_specs=VMEM,
        name="unpack",
    )(index, *pieces)


def attend_kernel(shape, tables_ref, *refs):
    groups, local, cubes, heads, first, count, picks, head_size, query_bases, store_bases = shape
    queries = refs[:groups]
    stores = refs[groups : groups + len(store_bases)]
    outs = refs[groups + len(store_bases) : 2 * groups + len(store_bases)]
    (
        held,
        pool_mask,
        pooled_keys,
        pooled_values,
        query_all,
        gate_columns,
        coarse_part,
        scores_buffer,
        weights_buffer,
        mixed_all,
        sems,
    ) = refs[2 * groups + len(store_bases) :]
    tokens = local * CUBE
    units = groups * local
    slots = held.shape[0]
    scale = LOG2E / math.sqrt(head_size)
    tile_rows = pool_mask.shape[1]
    tile_blocks = pool_mask.shape[0] // 2
    tiles = held.shape[1] // tile_rows

    def copies(head):
        slot = head % slots
        row, result = 0, []
        for i, (store, base) in enumerate(zip(stores, store_bases)):
            rows = store.shape[0]
            source = store.at[:, pl.ds(base + head * head_size, head_size)]
            target = held.at[slot, pl.ds(row, rows), :]
            result.append(pltpu.make_async_copy(source, target, sems.at[slot, i]))
            row += rows
        return result

    for head in range(min(slots, count)):
        for copy in copies(head):
            copy.start()
    home = tables_ref[cubes + units * heads * picks]
    mask_block = lax.broadcasted_iota(jnp.int32, pool_mask.shape, 0)
    is_value = mask_block >= tile_blocks
    mask_block = jnp.where(is_value, mask_block - tile_blocks, mask_block)
    mask_start = (mask_block + lax.div(mask_block, local) * local) * CUBE
    mask_start = jnp.where(is_value, mask_start + tokens, mask_start)
    mask_row = lax.broadcasted_iota(jnp.int32, pool_mask.shape, 1)
    inside = jnp.logical_and(mask_row >= mask_start, mask_row < mask_start + CUBE)
    pool_mask[...] = jnp.where(inside, 1.0, 0.0).astype(jnp.bfloat16)
    for group in range(groups):
        base = query_bases[group]
        rows = slice(group * tokens, (group + 1) * tokens)
        query_all[rows, :] = queries[group][:tokens, base : base + count * head_size]
    ones = jnp.ones((picks * CUBE, head_size), jnp.bfloat16)

    for head in range(count):
        slot = head % slots
        columns = slice(head * head_size, (head + 1) * head_size)
        for group in range(groups):
            base = query_bases[group] + head * head_size
            gate_rows = queries[group][tokens : tokens + GATE_ROWS, base : base + head_size]
            gate_rows = jax.nn.sigmoid(gate_rows.astype(jnp.float32))
            gate_columns[group * tokens : (group + 1) * tokens, :] = jnp.transpose(gate_rows)
        for copy in copies(head):
            copy.wait()
        for tile in range(0, tiles, 2):
            pair = [held[slot, t * tile_rows : (t + 1) * tile_rows, :] for t in (tile, tile + 1)]
            sums = jnp.dot(
                pool_mask[...], jnp.concatenate(pair, axis=1), preferred_element_type=jnp.float32
            )
            means = (sums * (1.0 / CUBE)).astype(jnp.bfloat16)
            for t in (0, 1):
                rows = slice((tile + t) * tile_blocks, (tile + t + 1) * tile_blocks)
                part = means[:, t * head_size : (t + 1) * head_size]
                pooled_keys[rows, :] = part[:tile_blocks]
                pooled_values[rows, :head_size] = part[tile_blocks:]
        pooled_values[:, head_size:] = ones[:cubes] if cubes <= picks * CUBE else jnp.ones(
            (cubes, head_size), jnp.bfloat16
        )
        for group in range(groups):
            rows = slice(group * tokens, (group + 1) * tokens)
            scores = lax.dot_general(
                query_all[rows, columns],
                pooled_keys[...],
                TRANSPOSED,
                preferred_element_type=jnp.float32,
            )
            top = jnp.max(scores, axis=1, keepdims=True)
            weights = jnp.exp2((scores - top) * scale).astype(jnp.bfloat16)
            sums = jnp.dot(weights, pooled_values[...], preferred_element_type=jnp.float32)
            gate = gate_columns[rows, 0:1]
            coarse_part[rows, :] = sums[:, :head_size] * (gate / sums[:, head_size:])

        def unit_starts(unit):
            block = ((home ^ (unit // local)) * local + unit % local) * heads
            base = cubes + (block + first + head) * picks
            return [
                pl.multiple_of(tables_ref[tables_ref[base + pick]], CUBE) for pick in range(picks)
            ]

        def score_stage(unit):
            keys = [held[slot, pl.ds(start, CUBE), :] for start in unit_starts(unit)]
            scores_buffer[unit % 2] = lax.dot_general(
                query_all[unit * CUBE : (unit + 1) * CUBE, columns],
                jnp.concatenate(keys, axis=0),
                TRANSPOSED,
                preferred_element_type=jnp.float32,
            )

        def weight_stage(unit):
            scores = scores_buffer[unit % 2]
            top = jnp.max(scores, axis=1, keepdims=True)
            weights_buffer[unit % 2] = jnp.exp2((scores - top) * scale).astype(jnp.bfloat16)

        def value_stage(unit):
            values = [held[slot, pl.ds(start + tokens, CUBE), :] for start in unit_starts(unit)]
            values = jnp.concatenate((jnp.concatenate(values, axis=0), ones), axis=1)
            sums = jnp.dot(weights_buffer[unit % 2], values, preferred_element_type=jnp.float32)
            rows = slice(unit * CUBE, (unit + 1) * CUBE)
            gate = gate_columns[rows, 1:2]
            fine = sums[:, :head_size] * (gate / sums[:, head_size:])
            mixed_all[rows, columns] = (coarse_part[rows, :] + fine).astype(jnp.bfloat16)

        for unit in range(units + 2):
            if unit >= 2:
                value_stage(unit - 2)
            if 1 <= unit <= units:
                weight_stage(unit - 1)
            if unit < units:
                score_stage(unit)
        for group in range(groups):
            rows = slice(group * tokens, (group + 1) * tokens)
            outs[group][:, columns] = mixed_all[rows, columns]
        if head + slots < count:
            for copy in copies(head + slots):
                copy.start()


def attend(tables, queries, query_bases, stores, store_bases, sizes):
    local, cubes, heads, first, count, picks, head_size = sizes
    groups = len(queries)
    tokens = local * CUBE
    rows_all = 2 * cubes * CUBE
    tile_rows = min(POOL_ROWS, rows_all // 2)
    slots = max(2, min(count, HELD_BYTES // (2 * rows_all * head_size)))
    shape = (
        groups,
        local,
        cubes,
        heads,
        first,
        count,
        picks,
        head_size,
        tuple(query_bases),
        tuple(store_bases),
    )
    out = jax.ShapeDtypeStruct((tokens, count * head_size), jnp.bfloat16)
    units = groups * local
    return pl.pallas_call(
        functools.partial(attend_kernel, shape),
        out_shape=[out] * groups,
        in_specs=[SMEM] + [VMEM] * groups + [ANY] * len(stores),
        out_specs=[VMEM] * groups,
        scratch_shapes=[
            pltpu.VMEM((slots, rows_all, head_size), jnp.bfloat16),
            pltpu.VMEM((tile_rows // CUBE, tile_rows), jnp.bfloat16),
            pltpu.VMEM((cubes, head_size), jnp.bfloat16),
            pltpu.VMEM((cubes, 2 * head_size), jnp.bfloat16),
            pltpu.VMEM((groups * tokens, count * head_size), jnp.bfloat16),
            pltpu.VMEM((groups * tokens, GATE_ROWS), jnp.float32),
            pltpu.VMEM((groups * tokens, head_size), jnp.float32),
            pltpu.VMEM((2, CUBE, picks * CUBE), jnp.float32),
            pltpu.VMEM((2, CUBE, picks * CUBE), jnp.bfloat16),
            pltpu.VMEM((groups * tokens, count * head_size), jnp.bfloat16),
            pltpu.SemaphoreType.DMA((slots, len(stores))),
        ],
        cost_estimate=pl.CostEstimate(
            flops=4 * units * count * CUBE * CUBE * picks * head_size,
            bytes_accessed=2 * rows_all * count * head_size,
            transcendentals=units * count * CUBE * CUBE * picks,
        ),
        compiler_params=pltpu.CompilerParams(
            vmem_limit_bytes=2 * slots * rows_all * head_size + (10 << 20)
        ),
        name="attend",
    )(tables, *queries, *stores)


def body(query_rows, key_rows, value_rows, gate_logits, selection, cube_ids):
    devices = lax.axis_size("cubes")
    tokens, width = query_rows.shape
    heads_all = gate_logits.shape[1] // 2
    head_size = width // heads_all
    if tokens != head_size:
        raise ValueError("gate rows")
    local = tokens // CUBE
    cubes = cube_ids.shape[0]
    picks = selection.shape[2]
    common = math.gcd(heads_all, devices)
    groups = common & -common
    ring = devices // groups
    heads = heads_all // groups
    group_width = heads * head_size
    self_index = lax.axis_index("cubes")
    home = self_index // ring
    place = self_index % ring

    counts = CHUNKS if sum(CHUNKS) == heads else (heads,)
    firsts = [sum(counts[:i]) for i in range(len(counts))]
    spans = [(first * head_size, count * head_size) for first, count in zip(firsts, counts)]

    def over_groups(value, relative):
        pairs = [(i, i ^ (relative * ring)) for i in range(devices)]
        return lax.ppermute(value, "cubes", pairs)

    def over_ring(value, step):
        return lax.ppermute(value, "cubes", [(i, i ^ step) for i in range(devices)])

    steps = [1 << bit for bit in range(ring.bit_length() - 2, -1, -1)]

    def gather(value):
        stores = [value]
        for number, step in enumerate(steps):
            stores = stores + [over_ring(store, step) for store in stores]
            if number + 2 < len(steps):
                stores = [jnp.concatenate(stores, axis=0)]
        return stores

    index = home.astype(jnp.int32).reshape(1)
    order = [*range(groups - 1, 1, -1), 1]
    whole = (0, group_width)
    gate_rows = jnp.transpose(gate_logits).reshape(2, heads_all * tokens)
    gate_rows = jnp.pad(gate_rows, ((0, GATE_ROWS - 2), (0, 0)))

    sent = [(r, *whole) for r in order + [0]]
    keys_sent = pack(index, [((key_rows, value_rows), sent)], group_width)
    queries_sent = pack(index, [((query_rows, gate_rows), sent)], group_width)

    cube_range = jnp.arange(cubes, dtype=jnp.int32)
    device_of = cube_range // local
    offset = jnp.bitwise_xor(device_of % ring, place)
    relative = jnp.bitwise_xor(device_of // ring, home)
    slot = jnp.zeros_like(offset)
    for number, step in enumerate(steps):
        slot = slot + jnp.where(jnp.bitwise_and(offset, step) > 0, 1 << number, 0)
    piece = relative * ring + slot
    start = piece * (2 * tokens) + (cube_range % local) * CUBE
    row_of_cube = jnp.sum(
        jnp.where(cube_ids[None, :] == cube_range[:, None], start[None, :], 0), axis=1
    )
    chosen = selection.reshape(groups, ring, local, heads_all, picks)
    chosen = lax.dynamic_slice(
        chosen, (0, place, 0, home * heads, 0), (groups, 1, local, heads, picks)
    )
    tables = jnp.concatenate((row_of_cube, chosen.reshape(-1), index)).astype(jnp.int32)

    arrived = {}
    for r, value in zip(order, keys_sent):
        arrived[r] = over_groups(value, r)
    arrived[0] = keys_sent[-1]
    queries = {0: queries_sent[-1]}
    for r, value in zip(order, queries_sent):
        queries[r] = over_groups(value, r)
    stores = {}
    for r in [0] + order:
        stores[r] = gather(arrived[r])
    stores = [store for r in range(groups) for store in stores[r]]

    pieces, placed = [], []
    for number, (begin, size) in enumerate(spans):
        outs = attend(
            tables,
            [queries[r] for r in range(groups)],
            [begin] * groups,
            stores,
            [begin] * len(stores),
            (local, cubes, heads, firsts[number], counts[number], picks, head_size),
        )
        pieces.append(outs[0])
        for r in order:
            pieces.append(over_groups(outs[r], r))
        placed += [(r, begin, size) for r in [0] + order]
    return unpack(index, pieces, placed, group_width, width)


def solution(mesh):
    placed = (
        P(("groups", "cubes"), None),
        P(("groups", "cubes"), None),
        P(("groups", "cubes"), None),
        P(("groups", "cubes"), None),
        P("groups", None, None),
        P("groups"),
    )

    return jax.shard_map(
        body, mesh=mesh, in_specs=placed, out_specs=P(("groups", "cubes"), None), check_vma=False
    )
```

```python
import functools
import math

import jax
import jax.numpy as jnp
from jax import lax
from jax.experimental import pallas as pl
from jax.experimental.pallas import tpu as pltpu
from jax.sharding import PartitionSpec as P


CUBE = 64
GATE_ROWS = 8
CHUNKS = (3, 2)
POOL_ROWS = 1024
HELD_BYTES = 8 << 20
SMALL_VMEM = 12 << 20
LOG2E = 1.4426950408889634

VMEM = pl.BlockSpec(memory_space=pltpu.VMEM)
SMEM = pl.BlockSpec(memory_space=pltpu.SMEM)
ANY = pl.BlockSpec(memory_space=pl.ANY)
TRANSPOSED = (((1,), (1,)), ((), ()))


def pack_kernel(jobs, width, index_ref, *refs):
    sources = refs[: 1 + max(max(rows) for rows, _ in jobs)]
    outputs = iter(refs[len(sources) :])
    for numbers, spans in jobs:
        for relative, begin, size in spans:
            head_group = index_ref[0] ^ relative
            columns = pl.ds(pl.multiple_of(head_group * width + begin, 128), size)
            out, row = next(outputs), 0
            for number in numbers:
                rows = sources[number].shape[0]
                out[row : row + rows, :] = sources[number][:, columns]
                row += rows


def pack(index, jobs, width):
    operands, numbered, shapes = [], [], []
    for sources, spans in jobs:
        numbers = []
        for source in sources:
            known = [i for i, operand in enumerate(operands) if operand is source]
            numbers.append(known[0] if known else len(operands))
            if not known:
                operands.append(source)
        numbered.append((tuple(numbers), tuple(spans)))
        rows = sum(source.shape[0] for source in sources)
        shapes += [jax.ShapeDtypeStruct((rows, size), jnp.bfloat16) for _, _, size in spans]
    return pl.pallas_call(
        functools.partial(pack_kernel, tuple(numbered), width),
        out_shape=shapes,
        in_specs=[SMEM] + [VMEM] * len(operands),
        out_specs=[VMEM] * len(shapes),
        compiler_params=pltpu.CompilerParams(vmem_limit_bytes=SMALL_VMEM),
        name="pack",
    )(index, *operands)


def unpack_kernel(spans, width, index_ref, *refs):
    pieces, out = refs[:-1], refs[-1]
    for (relative, begin, size), piece in zip(spans, pieces):
        head_group = index_ref[0] ^ relative
        out[:, pl.ds(pl.multiple_of(head_group * width + begin, 128), size)] = piece[...]


def unpack(index, pieces, spans, width, columns):
    return pl.pallas_call(
        functools.partial(unpack_kernel, spans, width),
        out_shape=jax.ShapeDtypeStruct((pieces[0].shape[0], columns), jnp.bfloat16),
        in_specs=[SMEM] + [VMEM] * len(pieces),
        out_specs=VMEM,
        compiler_params=pltpu.CompilerParams(vmem_limit_bytes=SMALL_VMEM),
        name="unpack",
    )(index, *pieces)


def attend_kernel(shape, tables_ref, *refs):
    groups, local, cubes, heads, first, count, picks, head_size, query_bases, store_bases = shape
    queries = refs[:groups]
    stores = refs[groups : groups + len(store_bases)]
    outs = refs[groups + len(store_bases) : 2 * groups + len(store_bases)]
    (
        held,
        pool_mask,
        pooled_keys,
        pooled_values,
        query_all,
        gate_columns,
        coarse_part,
        scores_buffer,
        weights_buffer,
        mixed_all,
        sems,
    ) = refs[2 * groups + len(store_bases) :]
    tokens = local * CUBE
    units = groups * local
    slots = held.shape[0]
    scale = LOG2E / math.sqrt(head_size)
    tile_rows = pool_mask.shape[1]
    tile_blocks = pool_mask.shape[0] // 2
    tiles = held.shape[1] // tile_rows

    def copies(head):
        slot = head % slots
        row, result = 0, []
        for i, (store, base) in enumerate(zip(stores, store_bases)):
            rows = store.shape[0]
            source = store.at[:, pl.ds(base + head * head_size, head_size)]
            target = held.at[slot, pl.ds(row, rows), :]
            result.append(pltpu.make_async_copy(source, target, sems.at[slot, i]))
            row += rows
        return result

    for head in range(min(slots, count)):
        for copy in copies(head):
            copy.start()
    home = tables_ref[cubes + heads * picks * cubes]
    place = tables_ref[cubes + heads * picks * cubes + 1]
    ring = cubes // units
    mask_block = lax.broadcasted_iota(jnp.int32, pool_mask.shape, 0)
    is_value = mask_block >= tile_blocks
    mask_block = jnp.where(is_value, mask_block - tile_blocks, mask_block)
    mask_start = (mask_block + lax.div(mask_block, local) * local) * CUBE
    mask_start = jnp.where(is_value, mask_start + tokens, mask_start)
    mask_row = lax.broadcasted_iota(jnp.int32, pool_mask.shape, 1)
    inside = jnp.logical_and(mask_row >= mask_start, mask_row < mask_start + CUBE)
    pool_mask[...] = jnp.where(inside, 1.0, 0.0).astype(jnp.bfloat16)
    for group in range(groups):
        base = query_bases[group]
        rows = slice(group * tokens, (group + 1) * tokens)
        query_all[rows, :] = queries[group][:tokens, base : base + count * head_size]
    ones = jnp.ones((picks * CUBE, head_size), jnp.bfloat16)

    for head in range(count):
        slot = head % slots
        columns = slice(head * head_size, (head + 1) * head_size)
        for group in range(groups):
            base = query_bases[group] + head * head_size
            gate_rows = queries[group][tokens : tokens + GATE_ROWS, base : base + head_size]
            gate_rows = jax.nn.sigmoid(gate_rows.astype(jnp.float32))
            gate_columns[group * tokens : (group + 1) * tokens, :] = jnp.transpose(gate_rows)
        for copy in copies(head):
            copy.wait()
        for tile in range(0, tiles, 2):
            pair = [held[slot, t * tile_rows : (t + 1) * tile_rows, :] for t in (tile, tile + 1)]
            sums = jnp.dot(
                pool_mask[...], jnp.concatenate(pair, axis=1), preferred_element_type=jnp.float32
            )
            means = (sums * (1.0 / CUBE)).astype(jnp.bfloat16)
            for t in (0, 1):
                rows = slice((tile + t) * tile_blocks, (tile + t + 1) * tile_blocks)
                part = means[:, t * head_size : (t + 1) * head_size]
                pooled_keys[rows, :] = part[:tile_blocks]
                pooled_values[rows, :head_size] = part[tile_blocks:]
        pooled_values[:, head_size:] = ones[:cubes] if cubes <= picks * CUBE else jnp.ones(
            (cubes, head_size), jnp.bfloat16
        )
        for group in range(groups):
            rows = slice(group * tokens, (group + 1) * tokens)
            scores = lax.dot_general(
                query_all[rows, columns],
                pooled_keys[...],
                TRANSPOSED,
                preferred_element_type=jnp.float32,
            )
            top = jnp.max(scores, axis=1, keepdims=True)
            weights = jnp.exp2((scores - top) * scale).astype(jnp.bfloat16)
            sums = jnp.dot(weights, pooled_values[...], preferred_element_type=jnp.float32)
            gate = gate_columns[rows, 0:1]
            coarse_part[rows, :] = sums[:, :head_size] * (gate / sums[:, head_size:])

        def unit_starts(unit):
            block = ((home ^ (unit // local)) * ring + place) * local + unit % local
            base = cubes + (first + head) * picks * cubes + block
            return [
                pl.multiple_of(tables_ref[tables_ref[base + pick * cubes]], CUBE)
                for pick in range(picks)
            ]

        def score_stage(unit):
            keys = [held[slot, pl.ds(start, CUBE), :] for start in unit_starts(unit)]
            scores_buffer[unit % 2] = lax.dot_general(
                query_all[unit * CUBE : (unit + 1) * CUBE, columns],
                jnp.concatenate(keys, axis=0),
                TRANSPOSED,
                preferred_element_type=jnp.float32,
            )

        def weight_stage(unit):
            scores = scores_buffer[unit % 2]
            top = jnp.max(scores, axis=1, keepdims=True)
            weights_buffer[unit % 2] = jnp.exp2((scores - top) * scale).astype(jnp.bfloat16)

        def value_stage(unit):
            values = [held[slot, pl.ds(start + tokens, CUBE), :] for start in unit_starts(unit)]
            values = jnp.concatenate((jnp.concatenate(values, axis=0), ones), axis=1)
            sums = jnp.dot(weights_buffer[unit % 2], values, preferred_element_type=jnp.float32)
            rows = slice(unit * CUBE, (unit + 1) * CUBE)
            gate = gate_columns[rows, 1:2]
            fine = sums[:, :head_size] * (gate / sums[:, head_size:])
            mixed_all[rows, columns] = (coarse_part[rows, :] + fine).astype(jnp.bfloat16)

        for unit in range(units + 2):
            if unit >= 2:
                value_stage(unit - 2)
            if 1 <= unit <= units:
                weight_stage(unit - 1)
            if unit < units:
                score_stage(unit)
        for group in range(groups):
            rows = slice(group * tokens, (group + 1) * tokens)
            outs[group][:, columns] = mixed_all[rows, columns]
        if head + slots < count:
            for copy in copies(head + slots):
                copy.start()


def attend(tables, queries, query_bases, stores, store_bases, sizes):
    local, cubes, heads, first, count, picks, head_size = sizes
    groups = len(queries)
    tokens = local * CUBE
    rows_all = 2 * cubes * CUBE
    tile_rows = min(POOL_ROWS, rows_all // 2)
    slots = max(2, min(count, HELD_BYTES // (2 * rows_all * head_size)))
    shape = (
        groups,
        local,
        cubes,
        heads,
        first,
        count,
        picks,
        head_size,
        tuple(query_bases),
        tuple(store_bases),
    )
    out = jax.ShapeDtypeStruct((tokens, count * head_size), jnp.bfloat16)
    units = groups * local
    return pl.pallas_call(
        functools.partial(attend_kernel, shape),
        out_shape=[out] * groups,
        in_specs=[SMEM] + [VMEM] * groups + [ANY] * len(stores),
        out_specs=[VMEM] * groups,
        scratch_shapes=[
            pltpu.VMEM((slots, rows_all, head_size), jnp.bfloat16),
            pltpu.VMEM((tile_rows // CUBE, tile_rows), jnp.bfloat16),
            pltpu.VMEM((cubes, head_size), jnp.bfloat16),
            pltpu.VMEM((cubes, 2 * head_size), jnp.bfloat16),
            pltpu.VMEM((groups * tokens, count * head_size), jnp.bfloat16),
            pltpu.VMEM((groups * tokens, GATE_ROWS), jnp.float32),
            pltpu.VMEM((groups * tokens, head_size), jnp.float32),
            pltpu.VMEM((2, CUBE, picks * CUBE), jnp.float32),
            pltpu.VMEM((2, CUBE, picks * CUBE), jnp.bfloat16),
            pltpu.VMEM((groups * tokens, count * head_size), jnp.bfloat16),
            pltpu.SemaphoreType.DMA((slots, len(stores))),
        ],
        cost_estimate=pl.CostEstimate(
            flops=4 * units * count * CUBE * CUBE * picks * head_size,
            bytes_accessed=2 * rows_all * count * head_size,
            transcendentals=units * count * CUBE * CUBE * picks,
        ),
        compiler_params=pltpu.CompilerParams(
            vmem_limit_bytes=2 * slots * rows_all * head_size + (10 << 20)
        ),
        name="attend",
    )(tables, *queries, *stores)


def body(query_rows, key_rows, value_rows, gate_logits, selection, cube_ids):
    devices = lax.axis_size("cubes")
    tokens, width = query_rows.shape
    heads_all = gate_logits.shape[1] // 2
    head_size = width // heads_all
    if tokens != head_size:
        raise ValueError("gate rows")
    local = tokens // CUBE
    cubes = cube_ids.shape[0]
    picks = selection.shape[2]
    common = math.gcd(heads_all, devices)
    groups = common & -common
    ring = devices // groups
    heads = heads_all // groups
    group_width = heads * head_size
    self_index = lax.axis_index("cubes")
    home = self_index // ring
    place = self_index % ring

    counts = CHUNKS if sum(CHUNKS) == heads else (heads,)
    firsts = [sum(counts[:i]) for i in range(len(counts))]
    spans = [(first * head_size, count * head_size) for first, count in zip(firsts, counts)]

    def over_groups(value, relative):
        pairs = [(i, i ^ (relative * ring)) for i in range(devices)]
        return lax.ppermute(value, "cubes", pairs)

    def over_ring(value, step):
        return lax.ppermute(value, "cubes", [(i, i ^ step) for i in range(devices)])

    steps = [1 << bit for bit in range(ring.bit_length() - 2, -1, -1)]

    def gather(stores, skipped):
        for number, step in enumerate(steps):
            if number < skipped:
                continue
            stores = stores + [over_ring(store, step) for store in stores]
            if number + 2 < len(steps):
                stores = [jnp.concatenate(stores, axis=0)]
        return stores

    index = home.astype(jnp.int32).reshape(1)
    order = [*range(groups - 1, 1, -1), 1]
    whole = (0, group_width)
    gate_rows = jnp.transpose(gate_logits).reshape(2, heads_all * tokens)
    gate_rows = jnp.pad(gate_rows, ((0, GATE_ROWS - 2), (0, 0)))

    sent = [(0, *whole)] + [(r, *span) for span in spans for r in order]
    keys_sent = pack(index, [((key_rows, value_rows), sent)], group_width)
    queries_sent = pack(index, [((query_rows, gate_rows), sent)], group_width)

    cube_range = jnp.arange(cubes, dtype=jnp.int32)
    device_of = cube_range // local
    offset = jnp.bitwise_xor(device_of % ring, place)
    relative = jnp.bitwise_xor(device_of // ring, home)
    slot = jnp.zeros_like(offset)
    for number, step in enumerate(steps):
        slot = slot + jnp.where(jnp.bitwise_and(offset, step) > 0, 1 << number, 0)
    piece = jnp.where(relative == 0, slot, ring + slot * (groups - 1) + relative - 1)
    start = piece * (2 * tokens) + (cube_range % local) * CUBE
    row_of_cube = jnp.sum(
        jnp.where(cube_ids[None, :] == cube_range[:, None], start[None, :], 0), axis=1
    )
    chosen = jnp.transpose(selection, (1, 2, 0))
    chosen = lax.dynamic_slice(chosen, (home * heads, 0, 0), (heads, picks, cubes))
    tables = jnp.concatenate((row_of_cube, chosen.reshape(-1), index, place.reshape(1)))
    tables = tables.astype(jnp.int32)

    own_stores = gather([keys_sent[0]], 0)
    pieces, placed = [], []
    for c, (begin, size) in enumerate(spans):
        keys, queries, beside = {}, {}, {}
        for number, r in enumerate(order):
            keys[r] = over_groups(keys_sent[1 + c * len(order) + number], r)
            queries[r] = over_groups(queries_sent[1 + c * len(order) + number], r)
        for r in order if steps else []:
            beside[r] = over_ring(keys[r], steps[0])
        stores = [
            jnp.concatenate([part[r] for r in range(1, groups)], axis=0)
            for part in (keys, beside)
            if part
        ]
        if len(steps) > 2:
            stores = [jnp.concatenate(stores, axis=0)]
        stores = gather(stores, 1)
        outs = attend(
            tables,
            [queries_sent[0]] + [queries[r] for r in range(1, groups)],
            [begin] + [0] * (groups - 1),
            own_stores + stores,
            [begin] * len(own_stores) + [0] * len(stores),
            (local, cubes, heads, firsts[c], counts[c], picks, head_size),
        )
        pieces.append(outs[0])
        for r in order:
            pieces.append(over_groups(outs[r], r))
        placed += [(r, begin, size) for r in [0] + order]
    return unpack(index, pieces, placed, group_width, width)


def solution(mesh):
    placed = (
        P(("groups", "cubes"), None),
        P(("groups", "cubes"), None),
        P(("groups", "cubes"), None),
        P(("groups", "cubes"), None),
        P("groups", None, None),
        P("groups"),
    )

    return jax.shard_map(
        body, mesh=mesh, in_specs=placed, out_specs=P(("groups", "cubes"), None), check_vma=False
    )
```

```python
import functools
import math

import jax
import jax.numpy as jnp
from jax import lax
from jax.experimental import pallas as pl
from jax.experimental.pallas import tpu as pltpu
from jax.sharding import PartitionSpec as P


CUBE = 64
GATE_ROWS = 8
CHUNKS = ((2, 1), (2,))
POOL_ROWS = 1024
HELD_BYTES = 8 << 20
SMALL_VMEM = 12 << 20
LOG2E = 1.4426950408889634

VMEM = pl.BlockSpec(memory_space=pltpu.VMEM)
SMEM = pl.BlockSpec(memory_space=pltpu.SMEM)
ANY = pl.BlockSpec(memory_space=pl.ANY)
HBM = pl.BlockSpec(memory_space=pltpu.MemorySpace.HBM)
TRANSPOSED = (((1,), (1,)), ((), ()))


def pack_kernel(jobs, width, index_ref, *refs):
    sources, refs, sems = refs[: 1 + max(max(rows) for rows, _ in jobs)], refs[:-1], refs[-1]
    outputs = iter(refs[len(sources) :])
    copies = []
    for numbers, spans in jobs:
        for relative, begin, size in spans:
            head_group = index_ref[0] ^ relative
            columns = pl.ds(pl.multiple_of(head_group * width + begin, 128), size)
            out, row = next(outputs), 0
            for number in numbers:
                rows = sources[number].shape[0]
                source, target = sources[number].at[:, columns], out.at[pl.ds(row, rows), :]
                copies.append(pltpu.make_async_copy(source, target, sems.at[len(copies)]))
                copies[-1].start()
                row += rows
    for copy in copies:
        copy.wait()


def pack(index, jobs, width):
    operands, numbered, shapes = [], [], []
    for sources, spans in jobs:
        numbers = []
        for source in sources:
            known = [i for i, operand in enumerate(operands) if operand is source]
            numbers.append(known[0] if known else len(operands))
            if not known:
                operands.append(source)
        numbered.append((tuple(numbers), tuple(spans)))
        rows = sum(source.shape[0] for source in sources)
        shapes += [jax.ShapeDtypeStruct((rows, size), jnp.bfloat16) for _, _, size in spans]
    return pl.pallas_call(
        functools.partial(pack_kernel, tuple(numbered), width),
        out_shape=shapes,
        in_specs=[SMEM] + [HBM] * len(operands),
        out_specs=[VMEM] * len(shapes),
        scratch_shapes=[pltpu.SemaphoreType.DMA((sum(len(n) * len(p) for n, p in numbered),))],
        compiler_params=pltpu.CompilerParams(vmem_limit_bytes=SMALL_VMEM),
        name="pack",
    )(index, *operands)


def unpack_kernel(spans, width, index_ref, *refs):
    pieces, out = refs[:-1], refs[-1]
    for (relative, begin, size), piece in zip(spans, pieces):
        head_group = index_ref[0] ^ relative
        out[:, pl.ds(pl.multiple_of(head_group * width + begin, 128), size)] = piece[...]


def unpack(index, pieces, spans, width, columns):
    return pl.pallas_call(
        functools.partial(unpack_kernel, spans, width),
        out_shape=jax.ShapeDtypeStruct((pieces[0].shape[0], columns), jnp.bfloat16),
        in_specs=[SMEM] + [VMEM] * len(pieces),
        out_specs=VMEM,
        compiler_params=pltpu.CompilerParams(vmem_limit_bytes=SMALL_VMEM),
        name="unpack",
    )(index, *pieces)


def attend_kernel(shape, tables_ref, *refs):
    groups, local, cubes, heads, first, count, picks, head_size, query_bases, store_bases = shape
    queries = refs[:groups]
    stores = refs[groups : groups + len(store_bases)]
    outs = refs[groups + len(store_bases) : 2 * groups + len(store_bases)]
    (
        held,
        pool_mask,
        pooled_keys,
        pooled_values,
        query_all,
        gate_columns,
        coarse_part,
        scores_buffer,
        weights_buffer,
        mixed_all,
        sems,
    ) = refs[2 * groups + len(store_bases) :]
    tokens = local * CUBE
    units = groups * local
    slots = held.shape[0]
    scale = LOG2E / math.sqrt(head_size)
    tile_rows = pool_mask.shape[1]
    tile_blocks = pool_mask.shape[0] // 2
    tiles = held.shape[1] // tile_rows

    def copies(head):
        slot = head % slots
        row, result = 0, []
        for i, (store, base) in enumerate(zip(stores, store_bases)):
            rows = store.shape[0]
            source = store.at[:, pl.ds(base + head * head_size, head_size)]
            target = held.at[slot, pl.ds(row, rows), :]
            result.append(pltpu.make_async_copy(source, target, sems.at[slot, i]))
            row += rows
        return result

    for head in range(min(slots, count)):
        for copy in copies(head):
            copy.start()
    home = tables_ref[cubes + heads * picks * cubes]
    place = tables_ref[cubes + heads * picks * cubes + 1]
    ring = cubes // units
    mask_block = lax.broadcasted_iota(jnp.int32, pool_mask.shape, 0)
    is_value = mask_block >= tile_blocks
    mask_block = jnp.where(is_value, mask_block - tile_blocks, mask_block)
    mask_start = (mask_block + lax.div(mask_block, local) * local) * CUBE
    mask_start = jnp.where(is_value, mask_start + tokens, mask_start)
    mask_row = lax.broadcasted_iota(jnp.int32, pool_mask.shape, 1)
    inside = jnp.logical_and(mask_row >= mask_start, mask_row < mask_start + CUBE)
    pool_mask[...] = jnp.where(inside, 1.0, 0.0).astype(jnp.bfloat16)
    for group in range(groups):
        base = query_bases[group]
        rows = slice(group * tokens, (group + 1) * tokens)
        query_all[rows, :] = queries[group][:tokens, base : base + count * head_size]
    ones = jnp.ones((picks * CUBE, head_size), jnp.bfloat16)

    for head in range(count):
        slot = head % slots
        columns = slice(head * head_size, (head + 1) * head_size)
        for group in range(groups):
            base = query_bases[group] + head * head_size
            gate_rows = queries[group][tokens : tokens + GATE_ROWS, base : base + head_size]
            gate_rows = jax.nn.sigmoid(gate_rows.astype(jnp.float32))
            gate_columns[group * tokens : (group + 1) * tokens, :] = jnp.transpose(gate_rows)
        for copy in copies(head):
            copy.wait()
        for tile in range(0, tiles, 2):
            pair = [held[slot, t * tile_rows : (t + 1) * tile_rows, :] for t in (tile, tile + 1)]
            sums = jnp.dot(
                pool_mask[...], jnp.concatenate(pair, axis=1), preferred_element_type=jnp.float32
            )
            means = (sums * (1.0 / CUBE)).astype(jnp.bfloat16)
            for t in (0, 1):
                rows = slice((tile + t) * tile_blocks, (tile + t + 1) * tile_blocks)
                part = means[:, t * head_size : (t + 1) * head_size]
                pooled_keys[rows, :] = part[:tile_blocks]
                pooled_values[rows, :head_size] = part[tile_blocks:]
        pooled_values[:, head_size:] = ones[:cubes] if cubes <= picks * CUBE else jnp.ones(
            (cubes, head_size), jnp.bfloat16
        )
        for group in range(groups):
            rows = slice(group * tokens, (group + 1) * tokens)
            scores = lax.dot_general(
                query_all[rows, columns],
                pooled_keys[...],
                TRANSPOSED,
                preferred_element_type=jnp.float32,
            )
            top = jnp.max(scores, axis=1, keepdims=True)
            weights = jnp.exp2((scores - top) * scale).astype(jnp.bfloat16)
            sums = jnp.dot(weights, pooled_values[...], preferred_element_type=jnp.float32)
            gate = gate_columns[rows, 0:1]
            coarse_part[rows, :] = sums[:, :head_size] * (gate / sums[:, head_size:])

        def unit_starts(unit):
            block = ((home ^ (unit // local)) * ring + place) * local + unit % local
            base = cubes + (first + head) * picks * cubes + block
            return [
                pl.multiple_of(tables_ref[tables_ref[base + pick * cubes]], CUBE)
                for pick in range(picks)
            ]

        def score_stage(unit):
            keys = [held[slot, pl.ds(start, CUBE), :] for start in unit_starts(unit)]
            scores_buffer[unit % 2] = lax.dot_general(
                query_all[unit * CUBE : (unit + 1) * CUBE, columns],
                jnp.concatenate(keys, axis=0),
                TRANSPOSED,
                preferred_element_type=jnp.float32,
            )

        def weight_stage(unit):
            scores = scores_buffer[unit % 2]
            top = jnp.max(scores, axis=1, keepdims=True)
            weights_buffer[unit % 2] = jnp.exp2((scores - top) * scale).astype(jnp.bfloat16)

        def value_stage(unit):
            values = [held[slot, pl.ds(start + tokens, CUBE), :] for start in unit_starts(unit)]
            values = jnp.concatenate((jnp.concatenate(values, axis=0), ones), axis=1)
            sums = jnp.dot(weights_buffer[unit % 2], values, preferred_element_type=jnp.float32)
            rows = slice(unit * CUBE, (unit + 1) * CUBE)
            gate = gate_columns[rows, 1:2]
            fine = sums[:, :head_size] * (gate / sums[:, head_size:])
            mixed_all[rows, columns] = (coarse_part[rows, :] + fine).astype(jnp.bfloat16)

        for unit in range(units + 2):
            if unit >= 2:
                value_stage(unit - 2)
            if 1 <= unit <= units:
                weight_stage(unit - 1)
            if unit < units:
                score_stage(unit)
        for group in range(groups):
            rows = slice(group * tokens, (group + 1) * tokens)
            outs[group][:, columns] = mixed_all[rows, columns]
        if head + slots < count:
            for copy in copies(head + slots):
                copy.start()


def attend(tables, queries, query_bases, stores, store_bases, sizes):
    local, cubes, heads, first, count, picks, head_size = sizes
    groups = len(queries)
    tokens = local * CUBE
    rows_all = 2 * cubes * CUBE
    tile_rows = min(POOL_ROWS, rows_all // 2)
    slots = max(2, min(count, HELD_BYTES // (2 * rows_all * head_size)))
    shape = (
        groups,
        local,
        cubes,
        heads,
        first,
        count,
        picks,
        head_size,
        tuple(query_bases),
        tuple(store_bases),
    )
    out = jax.ShapeDtypeStruct((tokens, count * head_size), jnp.bfloat16)
    units = groups * local
    return pl.pallas_call(
        functools.partial(attend_kernel, shape),
        out_shape=[out] * groups,
        in_specs=[SMEM] + [VMEM] * groups + [ANY] * len(stores),
        out_specs=[VMEM] * groups,
        scratch_shapes=[
            pltpu.VMEM((slots, rows_all, head_size), jnp.bfloat16),
            pltpu.VMEM((tile_rows // CUBE, tile_rows), jnp.bfloat16),
            pltpu.VMEM((cubes, head_size), jnp.bfloat16),
            pltpu.VMEM((cubes, 2 * head_size), jnp.bfloat16),
            pltpu.VMEM((groups * tokens, count * head_size), jnp.bfloat16),
            pltpu.VMEM((groups * tokens, GATE_ROWS), jnp.float32),
            pltpu.VMEM((groups * tokens, head_size), jnp.float32),
            pltpu.VMEM((2, CUBE, picks * CUBE), jnp.float32),
            pltpu.VMEM((2, CUBE, picks * CUBE), jnp.bfloat16),
            pltpu.VMEM((groups * tokens, count * head_size), jnp.bfloat16),
            pltpu.SemaphoreType.DMA((slots, len(stores))),
        ],
        cost_estimate=pl.CostEstimate(
            flops=4 * units * count * CUBE * CUBE * picks * head_size,
            bytes_accessed=2 * rows_all * count * head_size,
            transcendentals=units * count * CUBE * CUBE * picks,
        ),
        compiler_params=pltpu.CompilerParams(
            vmem_limit_bytes=2 * slots * rows_all * head_size + (10 << 20)
        ),
        name="attend",
    )(tables, *queries, *stores)


def body(query_rows, key_rows, value_rows, gate_logits, selection, cube_ids):
    devices = lax.axis_size("cubes")
    tokens, width = query_rows.shape
    heads_all = gate_logits.shape[1] // 2
    head_size = width // heads_all
    if tokens != head_size:
        raise ValueError("gate rows")
    local = tokens // CUBE
    cubes = cube_ids.shape[0]
    picks = selection.shape[2]
    common = math.gcd(heads_all, devices)
    groups = common & -common
    ring = devices // groups
    heads = heads_all // groups
    group_width = heads * head_size
    self_index = lax.axis_index("cubes")
    home = self_index // ring
    place = self_index % ring

    chunks = CHUNKS if sum(map(sum, CHUNKS)) == heads else ((heads,),)
    counts = [sum(parts) for parts in chunks]
    firsts = [sum(counts[:i]) for i in range(len(counts))]
    spans = [(first * head_size, count * head_size) for first, count in zip(firsts, counts)]

    def over_groups(value, relative):
        pairs = [(i, i ^ (relative * ring)) for i in range(devices)]
        return lax.ppermute(value, "cubes", pairs)

    def over_ring(value, step):
        return lax.ppermute(value, "cubes", [(i, i ^ step) for i in range(devices)])

    steps = [1 << bit for bit in range(ring.bit_length() - 2, -1, -1)]

    def gather(stores, skipped):
        for number, step in enumerate(steps):
            if number < skipped:
                continue
            stores = stores + [over_ring(store, step) for store in stores]
            if number + 2 < len(steps):
                stores = [jnp.concatenate(stores, axis=0)]
        return stores

    index = home.astype(jnp.int32).reshape(1)
    order = [*range(groups - 1, 1, -1), 1]
    whole = (0, group_width)
    gate_rows = jnp.transpose(gate_logits).reshape(2, heads_all * tokens)
    gate_rows = jnp.pad(gate_rows, ((0, GATE_ROWS - 2), (0, 0)))

    sent = [(0, *whole)] + [(r, *span) for span in spans for r in order]
    keys_sent = pack(index, [((key_rows, value_rows), sent)], group_width)
    queries_sent = pack(index, [((query_rows, gate_rows), sent)], group_width)

    cube_range = jnp.arange(cubes, dtype=jnp.int32)
    device_of = cube_range // local
    offset = jnp.bitwise_xor(device_of % ring, place)
    relative = jnp.bitwise_xor(device_of // ring, home)
    slot = jnp.zeros_like(offset)
    for number, step in enumerate(steps):
        slot = slot + jnp.where(jnp.bitwise_and(offset, step) > 0, 1 << number, 0)
    piece = jnp.where(relative == 0, slot, ring + slot * (groups - 1) + relative - 1)
    start = piece * (2 * tokens) + (cube_range % local) * CUBE
    row_of_cube = jnp.sum(
        jnp.where(cube_ids[None, :] == cube_range[:, None], start[None, :], 0), axis=1
    )
    chosen = jnp.transpose(selection, (1, 2, 0))
    chosen = lax.dynamic_slice(chosen, (home * heads, 0, 0), (heads, picks, cubes))
    tables = jnp.concatenate((row_of_cube, chosen.reshape(-1), index, place.reshape(1)))
    tables = tables.astype(jnp.int32)

    own_stores = gather([keys_sent[0]], 0)
    pieces, placed = [], []
    for c, (begin, size) in enumerate(spans):
        keys, queries, beside = {}, {}, {}
        for number, r in enumerate(order):
            keys[r] = over_groups(keys_sent[1 + c * len(order) + number], r)
            queries[r] = over_groups(queries_sent[1 + c * len(order) + number], r)
        for r in order if steps else []:
            beside[r] = over_ring(keys[r], steps[0])
        stores = [
            jnp.concatenate([part[r] for r in range(1, groups)], axis=0)
            for part in (keys, beside)
            if part
        ]
        if len(steps) > 2:
            stores = [jnp.concatenate(stores, axis=0)]
        stores = gather(stores, 1)
        parts, offset = [], 0
        for count in chunks[c]:
            columns = offset * head_size
            outs = attend(
                tables,
                [queries_sent[0]] + [queries[r] for r in range(1, groups)],
                [begin + columns] + [columns] * (groups - 1),
                own_stores + stores,
                [begin + columns] * len(own_stores) + [columns] * len(stores),
                (local, cubes, heads, firsts[c] + offset, count, picks, head_size),
            )
            parts.append(outs)
            offset += count
        outs = [jnp.concatenate(part, axis=1) if len(part) > 1 else part[0] for part in zip(*parts)]
        pieces.append(outs[0])
        for r in order:
            pieces.append(over_groups(outs[r], r))
        placed += [(r, begin, size) for r in [0] + order]
    return unpack(index, pieces, placed, group_width, width)


def solution(mesh):
    placed = (
        P(("groups", "cubes"), None),
        P(("groups", "cubes"), None),
        P(("groups", "cubes"), None),
        P(("groups", "cubes"), None),
        P("groups", None, None),
        P("groups"),
    )

    return jax.shard_map(
        body, mesh=mesh, in_specs=placed, out_specs=P(("groups", "cubes"), None), check_vma=False
    )
```

```python
import functools
import math

import jax
import jax.numpy as jnp
from jax import lax
from jax.experimental import pallas as pl
from jax.experimental.pallas import tpu as pltpu
from jax.sharding import PartitionSpec as P


CUBE = 64
GATE_ROWS = 8
CHUNKS = ((2, 1), (2,))
POOL_ROWS = 1024
COARSE_ROWS = 512
HELD_BYTES = 8 << 20
SMALL_VMEM = 12 << 20
LOG2E = 1.4426950408889634

VMEM = pl.BlockSpec(memory_space=pltpu.VMEM)
SMEM = pl.BlockSpec(memory_space=pltpu.SMEM)
ANY = pl.BlockSpec(memory_space=pl.ANY)
HBM = pl.BlockSpec(memory_space=pltpu.MemorySpace.HBM)
TRANSPOSED = (((1,), (1,)), ((), ()))


def pack_kernel(jobs, width, index_ref, *refs):
    sources, refs, sems = refs[: 1 + max(max(rows) for rows, _ in jobs)], refs[:-1], refs[-1]
    outputs = iter(refs[len(sources) :])
    copies = []
    for numbers, spans in jobs:
        for relative, begin, size in spans:
            head_group = index_ref[0] ^ relative
            columns = pl.ds(pl.multiple_of(head_group * width + begin, 128), size)
            out, row = next(outputs), 0
            for number in numbers:
                rows = sources[number].shape[0]
                source, target = sources[number].at[:, columns], out.at[pl.ds(row, rows), :]
                copies.append(pltpu.make_async_copy(source, target, sems.at[len(copies)]))
                copies[-1].start()
                row += rows
    for copy in copies:
        copy.wait()


def pack(index, jobs, width):
    operands, numbered, shapes = [], [], []
    for sources, spans in jobs:
        numbers = []
        for source in sources:
            known = [i for i, operand in enumerate(operands) if operand is source]
            numbers.append(known[0] if known else len(operands))
            if not known:
                operands.append(source)
        numbered.append((tuple(numbers), tuple(spans)))
        rows = sum(source.shape[0] for source in sources)
        shapes += [jax.ShapeDtypeStruct((rows, size), jnp.bfloat16) for _, _, size in spans]
    return pl.pallas_call(
        functools.partial(pack_kernel, tuple(numbered), width),
        out_shape=shapes,
        in_specs=[SMEM] + [HBM] * len(operands),
        out_specs=[VMEM] * len(shapes),
        scratch_shapes=[pltpu.SemaphoreType.DMA((sum(len(n) * len(p) for n, p in numbered),))],
        compiler_params=pltpu.CompilerParams(vmem_limit_bytes=SMALL_VMEM),
        name="pack",
    )(index, *operands)


def unpack_kernel(spans, width, index_ref, *refs):
    pieces, out = refs[:-1], refs[-1]
    for (relative, begin, size), piece in zip(spans, pieces):
        head_group = index_ref[0] ^ relative
        out[:, pl.ds(pl.multiple_of(head_group * width + begin, 128), size)] = piece[...]


def unpack(index, pieces, spans, width, columns):
    return pl.pallas_call(
        functools.partial(unpack_kernel, spans, width),
        out_shape=jax.ShapeDtypeStruct((pieces[0].shape[0], columns), jnp.bfloat16),
        in_specs=[SMEM] + [VMEM] * len(pieces),
        out_specs=VMEM,
        compiler_params=pltpu.CompilerParams(vmem_limit_bytes=SMALL_VMEM),
        name="unpack",
    )(index, *pieces)


def attend_kernel(shape, tables_ref, *refs):
    groups, local, cubes, heads, first, count, picks, head_size, query_bases, store_bases = shape
    queries = refs[:groups]
    stores = refs[groups : groups + len(store_bases)]
    outs = refs[groups + len(store_bases) : 2 * groups + len(store_bases)]
    (
        held,
        pool_mask,
        pooled_keys,
        pooled_values,
        query_all,
        gate_columns,
        coarse_part,
        scores_buffer,
        weights_buffer,
        mixed_all,
        sems,
    ) = refs[2 * groups + len(store_bases) :]
    tokens = local * CUBE
    units = groups * local
    slots = held.shape[0]
    scale = LOG2E / math.sqrt(head_size)
    tile_rows = pool_mask.shape[1]
    tile_blocks = pool_mask.shape[0] // 2
    tiles = held.shape[1] // tile_rows

    def copies(head):
        slot = head % slots
        row, result = 0, []
        for i, (store, base) in enumerate(zip(stores, store_bases)):
            rows = store.shape[0]
            source = store.at[:, pl.ds(base + head * head_size, head_size)]
            target = held.at[slot, pl.ds(row, rows), :]
            result.append(pltpu.make_async_copy(source, target, sems.at[slot, i]))
            row += rows
        return result

    for head in range(min(slots, count)):
        for copy in copies(head):
            copy.start()
    home = tables_ref[cubes + heads * picks * cubes]
    place = tables_ref[cubes + heads * picks * cubes + 1]
    ring = cubes // units
    mask_block = lax.broadcasted_iota(jnp.int32, pool_mask.shape, 0)
    is_value = mask_block >= tile_blocks
    mask_block = jnp.where(is_value, mask_block - tile_blocks, mask_block)
    mask_start = (mask_block + lax.div(mask_block, local) * local) * CUBE
    mask_start = jnp.where(is_value, mask_start + tokens, mask_start)
    mask_row = lax.broadcasted_iota(jnp.int32, pool_mask.shape, 1)
    inside = jnp.logical_and(mask_row >= mask_start, mask_row < mask_start + CUBE)
    pool_mask[...] = jnp.where(inside, 1.0, 0.0).astype(jnp.bfloat16)
    for group in range(groups):
        base = query_bases[group]
        rows = slice(group * tokens, (group + 1) * tokens)
        query_all[rows, :] = queries[group][:tokens, base : base + count * head_size]
    ones = jnp.ones((picks * CUBE, head_size), jnp.bfloat16)

    for head in range(count):
        slot = head % slots
        columns = slice(head * head_size, (head + 1) * head_size)
        for group in range(groups):
            base = query_bases[group] + head * head_size
            gate_rows = queries[group][tokens : tokens + GATE_ROWS, base : base + head_size]
            gate_rows = jax.nn.sigmoid(gate_rows.astype(jnp.float32))
            gate_columns[group * tokens : (group + 1) * tokens, :] = jnp.transpose(gate_rows)
        for copy in copies(head):
            copy.wait()
        for tile in range(0, tiles, 2):
            pair = [held[slot, t * tile_rows : (t + 1) * tile_rows, :] for t in (tile, tile + 1)]
            sums = jnp.dot(
                pool_mask[...], jnp.concatenate(pair, axis=1), preferred_element_type=jnp.float32
            )
            means = (sums * (1.0 / CUBE)).astype(jnp.bfloat16)
            for t in (0, 1):
                rows = slice((tile + t) * tile_blocks, (tile + t + 1) * tile_blocks)
                part = means[:, t * head_size : (t + 1) * head_size]
                pooled_keys[rows, :] = part[:tile_blocks]
                pooled_values[rows, :head_size] = part[tile_blocks:]
        pooled_values[:, head_size:] = ones[:cubes] if cubes <= picks * CUBE else jnp.ones(
            (cubes, head_size), jnp.bfloat16
        )
        for row in range(0, groups * tokens, COARSE_ROWS):
            rows = slice(row, min(row + COARSE_ROWS, groups * tokens))
            scores = lax.dot_general(
                query_all[rows, columns],
                pooled_keys[...],
                TRANSPOSED,
                preferred_element_type=jnp.float32,
            )
            top = jnp.max(scores, axis=1, keepdims=True)
            weights = jnp.exp2((scores - top) * scale).astype(jnp.bfloat16)
            sums = jnp.dot(weights, pooled_values[...], preferred_element_type=jnp.float32)
            gate = gate_columns[rows, 0:1]
            coarse_part[rows, :] = sums[:, :head_size] * (gate / sums[:, head_size:])

        def unit_starts(unit):
            block = ((home ^ (unit // local)) * ring + place) * local + unit % local
            base = cubes + (first + head) * picks * cubes + block
            return [
                pl.multiple_of(tables_ref[tables_ref[base + pick * cubes]], CUBE)
                for pick in range(picks)
            ]

        def score_stage(unit):
            keys = [held[slot, pl.ds(start, CUBE), :] for start in unit_starts(unit)]
            scores_buffer[unit % 2] = lax.dot_general(
                query_all[unit * CUBE : (unit + 1) * CUBE, columns],
                jnp.concatenate(keys, axis=0),
                TRANSPOSED,
                preferred_element_type=jnp.float32,
            )

        def weight_stage(unit):
            scores = scores_buffer[unit % 2]
            top = jnp.max(scores, axis=1, keepdims=True)
            weights_buffer[unit % 2] = jnp.exp2((scores - top) * scale).astype(jnp.bfloat16)

        def value_stage(unit):
            values = [held[slot, pl.ds(start + tokens, CUBE), :] for start in unit_starts(unit)]
            values = jnp.concatenate((jnp.concatenate(values, axis=0), ones), axis=1)
            sums = jnp.dot(weights_buffer[unit % 2], values, preferred_element_type=jnp.float32)
            rows = slice(unit * CUBE, (unit + 1) * CUBE)
            gate = gate_columns[rows, 1:2]
            fine = sums[:, :head_size] * (gate / sums[:, head_size:])
            mixed_all[rows, columns] = (coarse_part[rows, :] + fine).astype(jnp.bfloat16)

        for unit in range(units + 2):
            if unit >= 2:
                value_stage(unit - 2)
            if 1 <= unit <= units:
                weight_stage(unit - 1)
            if unit < units:
                score_stage(unit)
        for group in range(groups):
            rows = slice(group * tokens, (group + 1) * tokens)
            outs[group][:, columns] = mixed_all[rows, columns]
        if head + slots < count:
            for copy in copies(head + slots):
                copy.start()


def attend(tables, queries, query_bases, stores, store_bases, sizes):
    local, cubes, heads, first, count, picks, head_size = sizes
    groups = len(queries)
    tokens = local * CUBE
    rows_all = 2 * cubes * CUBE
    tile_rows = min(POOL_ROWS, rows_all // 2)
    slots = max(2, min(count, HELD_BYTES // (2 * rows_all * head_size)))
    shape = (
        groups,
        local,
        cubes,
        heads,
        first,
        count,
        picks,
        head_size,
        tuple(query_bases),
        tuple(store_bases),
    )
    out = jax.ShapeDtypeStruct((tokens, count * head_size), jnp.bfloat16)
    units = groups * local
    return pl.pallas_call(
        functools.partial(attend_kernel, shape),
        out_shape=[out] * groups,
        in_specs=[SMEM] + [VMEM] * groups + [ANY] * len(stores),
        out_specs=[VMEM] * groups,
        scratch_shapes=[
            pltpu.VMEM((slots, rows_all, head_size), jnp.bfloat16),
            pltpu.VMEM((tile_rows // CUBE, tile_rows), jnp.bfloat16),
            pltpu.VMEM((cubes, head_size), jnp.bfloat16),
            pltpu.VMEM((cubes, 2 * head_size), jnp.bfloat16),
            pltpu.VMEM((groups * tokens, count * head_size), jnp.bfloat16),
            pltpu.VMEM((groups * tokens, GATE_ROWS), jnp.float32),
            pltpu.VMEM((groups * tokens, head_size), jnp.float32),
            pltpu.VMEM((2, CUBE, picks * CUBE), jnp.float32),
            pltpu.VMEM((2, CUBE, picks * CUBE), jnp.bfloat16),
            pltpu.VMEM((groups * tokens, count * head_size), jnp.bfloat16),
            pltpu.SemaphoreType.DMA((slots, len(stores))),
        ],
        cost_estimate=pl.CostEstimate(
            flops=4 * units * count * CUBE * CUBE * picks * head_size,
            bytes_accessed=2 * rows_all * count * head_size,
            transcendentals=units * count * CUBE * CUBE * picks,
        ),
        compiler_params=pltpu.CompilerParams(
            vmem_limit_bytes=2 * slots * rows_all * head_size + (10 << 20)
        ),
        name="attend",
    )(tables, *queries, *stores)


def body(query_rows, key_rows, value_rows, gate_logits, selection, cube_ids):
    devices = lax.axis_size("cubes")
    tokens, width = query_rows.shape
    heads_all = gate_logits.shape[1] // 2
    head_size = width // heads_all
    if tokens != head_size:
        raise ValueError("gate rows")
    local = tokens // CUBE
    cubes = cube_ids.shape[0]
    picks = selection.shape[2]
    common = math.gcd(heads_all, devices)
    groups = common & -common
    ring = devices // groups
    heads = heads_all // groups
    group_width = heads * head_size
    self_index = lax.axis_index("cubes")
    home = self_index // ring
    place = self_index % ring

    chunks = CHUNKS if sum(map(sum, CHUNKS)) == heads else ((heads,),)
    counts = [sum(parts) for parts in chunks]
    firsts = [sum(counts[:i]) for i in range(len(counts))]
    spans = [(first * head_size, count * head_size) for first, count in zip(firsts, counts)]

    def over_groups(value, relative):
        pairs = [(i, i ^ (relative * ring)) for i in range(devices)]
        return lax.ppermute(value, "cubes", pairs)

    def over_ring(value, step):
        return lax.ppermute(value, "cubes", [(i, i ^ step) for i in range(devices)])

    steps = [1 << bit for bit in range(ring.bit_length() - 2, -1, -1)]

    def gather(stores, skipped):
        for number, step in enumerate(steps):
            if number < skipped:
                continue
            stores = stores + [over_ring(store, step) for store in stores]
            if number + 2 < len(steps):
                stores = [jnp.concatenate(stores, axis=0)]
        return stores

    index = home.astype(jnp.int32).reshape(1)
    order = [*range(groups - 1, 1, -1), 1]
    whole = (0, group_width)
    gate_rows = jnp.transpose(gate_logits).reshape(2, heads_all * tokens)
    gate_rows = jnp.pad(gate_rows, ((0, GATE_ROWS - 2), (0, 0)))

    sent = [(0, *whole)] + [(r, *span) for span in spans for r in order]
    keys_sent = pack(index, [((key_rows, value_rows), sent)], group_width)
    queries_sent = pack(index, [((query_rows, gate_rows), sent)], group_width)

    cube_range = jnp.arange(cubes, dtype=jnp.int32)
    device_of = cube_range // local
    offset = jnp.bitwise_xor(device_of % ring, place)
    relative = jnp.bitwise_xor(device_of // ring, home)
    slot = jnp.zeros_like(offset)
    for number, step in enumerate(steps):
        slot = slot + jnp.where(jnp.bitwise_and(offset, step) > 0, 1 << number, 0)
    piece = jnp.where(relative == 0, slot, ring + slot * (groups - 1) + relative - 1)
    start = piece * (2 * tokens) + (cube_range % local) * CUBE
    row_of_cube = jnp.sum(
        jnp.where(cube_ids[None, :] == cube_range[:, None], start[None, :], 0), axis=1
    )
    chosen = jnp.transpose(selection, (1, 2, 0))
    chosen = lax.dynamic_slice(chosen, (home * heads, 0, 0), (heads, picks, cubes))
    tables = jnp.concatenate((row_of_cube, chosen.reshape(-1), index, place.reshape(1)))
    tables = tables.astype(jnp.int32)

    own_stores = gather([keys_sent[0]], 0)
    pieces, placed = [], []
    for c, (begin, size) in enumerate(spans):
        keys, queries, beside = {}, {}, {}
        for number, r in enumerate(order):
            keys[r] = over_groups(keys_sent[1 + c * len(order) + number], r)
            queries[r] = over_groups(queries_sent[1 + c * len(order) + number], r)
        for r in order if steps else []:
            beside[r] = over_ring(keys[r], steps[0])
        stores = [
            jnp.concatenate([part[r] for r in range(1, groups)], axis=0)
            for part in (keys, beside)
            if part
        ]
        if len(steps) > 2:
            stores = [jnp.concatenate(stores, axis=0)]
        stores = gather(stores, 1)
        parts, offset = [], 0
        for count in chunks[c]:
            columns = offset * head_size
            outs = attend(
                tables,
                [queries_sent[0]] + [queries[r] for r in range(1, groups)],
                [begin + columns] + [columns] * (groups - 1),
                own_stores + stores,
                [begin + columns] * len(own_stores) + [columns] * len(stores),
                (local, cubes, heads, firsts[c] + offset, count, picks, head_size),
            )
            parts.append(outs)
            offset += count
        outs = [jnp.concatenate(part, axis=1) if len(part) > 1 else part[0] for part in zip(*parts)]
        pieces.append(outs[0])
        for r in order:
            pieces.append(over_groups(outs[r], r))
        placed += [(r, begin, size) for r in [0] + order]
    return unpack(index, pieces, placed, group_width, width)


def solution(mesh):
    placed = (
        P(("groups", "cubes"), None),
        P(("groups", "cubes"), None),
        P(("groups", "cubes"), None),
        P(("groups", "cubes"), None),
        P("groups", None, None),
        P("groups"),
    )

    return jax.shard_map(
        body, mesh=mesh, in_specs=placed, out_specs=P(("groups", "cubes"), None), check_vma=False
    )
```
